256 devices in a mesh: src: 8 (over y, core), tgt: 32 (over z, x).
Axes of the slice: x: 4, y: 4, z: 8, core: 2. Of those that a mesh axis runs over, the one named last changes fastest.
Arguments:
- src_embed: bfloat16 [8192, 256], P('src'), may hold values from -128 to 128
- tgt_embed: bfloat16 [155648, 256], P('tgt'), may hold values from -1 to 1
- qwen_embed: bfloat16 [155648, 256], P('tgt'), may hold values from -6 to 6
- other_log: float32 [155648], P('tgt'), may hold values from -12 to -10
- src_counts: int32 [8192], P('src'), may hold values from 1 to 999
- tgt_counts: int32 [155648], P('tgt'), may hold values from 1 to 999
Outputs:
- transported: float32 [8192, 256], P(('src', 'tgt'))
The draws below stay inside these ranges and needn't reach their ends.
All inputs are finite; a program needn't handle non-finite values.
Results may differ from the reference program's by a relative error of at most 0.0034.
Values sent between devices are 32-bit elements; how exact they have to be, the bound alone decides.
A program may use at most 128 MiB of HBM per device.

```python
import jax
import jax.numpy as jnp
from jax import lax

COLS_DEV = 4864
EMB = 256
QDIM = 256
ITERS = 2
SLAB = 8192
VOCAB = 155648
N_TGT = 32


def target_values(key):
    base = jax.random.fold_in(key, 77)
    values = jnp.clip(jax.random.normal(jax.random.fold_in(base, 3), (VOCAB, EMB)), -6.0, 6.0) / jnp.sqrt(EMB * 1.0)
    return jnp.clip(values, -1.0, 1.0)


def draw_tgt_embed(key, part):
    return target_values(key).astype(jnp.bfloat16)


def draw_src_embed(key, part):
    base = jax.random.fold_in(key, 91)
    values = jnp.clip(jax.random.normal(jax.random.fold_in(base, 2), (SLAB, EMB)), -6.0, 6.0)
    return jnp.clip(values, -128.0, 128.0).astype(jnp.bfloat16)


def plant(drawn, stream_key, least, top_value):
    index_at = [jax.random.randint(jax.random.fold_in(stream_key, axis), (), 0, length) for axis, length in enumerate(drawn.shape)]
    main_axis = drawn.shape.index(max(drawn.shape))
    neighbour = index_at[:main_axis] + [(index_at[main_axis] + 1) % drawn.shape[main_axis]] + index_at[main_axis + 1:]
    return drawn.at[tuple(index_at)].set(least).at[tuple(neighbour)].set(top_value)


def block_levels(key, extent, cuts, least, high):
    factor_of = 1.0
    for axis_at, shards_of in cuts:
        heights = jax.random.uniform(jax.random.fold_in(jax.random.fold_in(key, 6), axis_at), (shards_of,), jnp.float32, least / len(cuts), high / len(cuts))
        factor_of = factor_of * jnp.repeat(jnp.exp(heights), extent[axis_at] // shards_of).reshape((-1,) + (1,) * (len(extent) - 1 - axis_at))
    return factor_of


def bell_draw(stream_key, shape, scale, limit, shards=(), kind=jnp.bfloat16):
    entries = jax.random.normal(stream_key, shape, jnp.float32) * scale
    if len(shards) > 0:
        entries = block_levels(stream_key, shape, shards, -0.22, 0.18) * entries
    return jnp.clip(entries, min=-limit, max=limit).astype(kind)


def setup_inputs(seed: int = 0) -> dict:
    key_of = jax.random.split(jax.random.key(seed), 7)
    return {
        "src_embed": draw_src_embed(jax.random.fold_in(key_of[6], 71), 0),
        "tgt_embed": draw_tgt_embed(jax.random.fold_in(key_of[6], 71), 0),
        "qwen_embed": bell_draw(key_of[2], (VOCAB, QDIM), 1.0, 6.0, ((0, 32),)),
        "other_log": jnp.clip(-12.0 + 2.0 * jax.random.uniform(key_of[3], (VOCAB,), jnp.float32) ** block_levels(key_of[3], (VOCAB,), ((0, 32),), -0.2, 0.2), -12.0, -10.0),
        "src_counts": plant(jax.random.randint(key_of[4], (SLAB,), 1, 1000), jax.random.fold_in(key_of[4], 1), 1, 999).astype(jnp.int32),
        "tgt_counts": plant(jax.random.randint(key_of[5], (VOCAB,), 1, 1000), jax.random.fold_in(key_of[5], 1), 1, 999).astype(jnp.int32),
    }


inv_temp = 4.0


def reference(src_embed, tgt_embed, qwen_embed, other_log, src_counts, tgt_counts):
    src_float = src_counts.astype(jnp.float32)
    tgt_float = tgt_counts.astype(jnp.float32)
    src_log = jnp.log(src_float) - jnp.log(jnp.sum(src_float))
    tgt_log = jnp.log(tgt_float) - jnp.log(jnp.sum(tgt_float))
    tgt_blocks = tgt_embed.reshape(N_TGT, COLS_DEV, EMB)
    qwen_blocks = qwen_embed.reshape(N_TGT, COLS_DEV, QDIM)
    other_blocks = other_log.reshape(N_TGT, COLS_DEV)
    tgt_log_blocks = tgt_log.reshape(N_TGT, COLS_DEV)

    def logits_of(block):
        return jnp.dot(src_embed, block.T, preferred_element_type=jnp.float32) * inv_temp

    col_pot = jnp.zeros((N_TGT, COLS_DEV), jnp.float32)
    row_pot = jnp.zeros((SLAB,), jnp.float32)
    for sweep in range(ITERS):
        def row_part(pair):
            block, potent = pair
            return jax.nn.logsumexp(logits_of(block) + potent[None, :], axis=1)

        parts = lax.map(row_part, (tgt_blocks, col_pot))
        row_pot = src_log - jax.nn.logsumexp(parts, axis=0)

        def col_part(block):
            return jax.nn.logsumexp(logits_of(block) + row_pot[:, None], axis=0)

        col_lse = lax.map(col_part, tgt_blocks)
        col_pot = tgt_log_blocks - jnp.logaddexp(col_lse, other_blocks)
    shift = row_pot - src_log

    def accumulate(total, triple):
        block, potent, qwen_block = triple
        weights = jnp.exp(shift[:, None] + potent[None, :] + logits_of(block)).astype(jnp.bfloat16)
        return total + jnp.dot(weights, qwen_block, preferred_element_type=jnp.float32), None

    start = jnp.zeros((SLAB, QDIM), jnp.float32)
    transported, unused = lax.scan(accumulate, start, (tgt_blocks, col_pot, qwen_blocks))
    return transported
```

```python
import functools
import math

import jax
import jax.numpy as jnp
from jax import lax
from jax.experimental import pallas as pl
from jax.experimental.pallas import tpu as pltpu
from jax.sharding import PartitionSpec as P

MESH = pl.DeviceIdType.MESH
LANES = 128
NX = 4
SCALE = 4.0 * math.log2(math.e)
NT = (((1,), (1,)), ((), ()))
NN = (((1,), (0,)), ((), ()))


def dot(a, b, dims):
    return lax.dot_general(a, b, dims, preferred_element_type=jnp.float32)


def kernel(
    n_src, n_tgt,
    src_hbm, tgt_hbm, qwen_hbm, other_ref, src_counts_ref, tgt_counts_ref,
    out_ref,
    src_v, tgt_v, qwen_v, qt_v, logit_v, kt_v, row_lhs, col_lhs,
    r1_send, r1_recv, c1_send, c1_recv, r2_send, r2_recv, c2_send, c2_recv,
    f_send, f_recv, g_send, g_recv,
    load_sem, send_sem, recv_sem,
):
    rows, emb = src_v.shape
    cols = tgt_v.shape[0]
    n_z = n_tgt // NX
    row_tiles, col_tiles = rows // LANES, cols // LANES
    owned = rows // n_tgt
    me_src, me_tgt = lax.axis_index("src"), lax.axis_index("tgt")
    me_z, me_x = me_tgt // NX, me_tgt % NX

    loads = [
        pltpu.make_async_copy(src_hbm, src_v, load_sem.at[0]),
        pltpu.make_async_copy(tgt_hbm, tgt_v, load_sem.at[1]),
        pltpu.make_async_copy(qwen_hbm, qwen_v, load_sem.at[2]),
    ]
    for load in loads:
        load.start()

    tgt_peers = [(me_src, (me_tgt + d) % n_tgt) for d in range(1, n_tgt)]
    src_peers = [((me_src + d) % n_src, me_tgt) for d in range(1, n_src)]
    barrier = pltpu.get_barrier_semaphore()
    for peer in tgt_peers + src_peers:
        pl.semaphore_signal(barrier, inc=1, device_id=peer, device_id_type=MESH)

    def start(send_ref, recv_ref, k, peers):
        for slot, peer in enumerate(peers):
            pltpu.make_async_remote_copy(
                src_ref=send_ref, dst_ref=recv_ref.at[slot],
                send_sem=send_sem.at[k], recv_sem=recv_sem.at[k],
                device_id=peer, device_id_type=MESH,
            ).start()

    def wait_recv(recv_ref, k):
        pltpu.make_async_copy(recv_ref, recv_ref, recv_sem.at[k]).wait()

    def wait_send(recv_ref, k):
        pltpu.make_async_copy(recv_ref, recv_ref, send_sem.at[k]).wait()

    loads[0].wait()
    loads[1].wait()
    width, block = 256, 608 if cols % 608 == 0 else cols
    n_blocks = cols // block
    for i in range(rows // width):
        lanes = pl.ds(i * width, width)
        src_part = src_v[lanes, :]

        def products(b, peak):
            js = pl.ds(pl.multiple_of(b * block, block), block)
            d = dot(tgt_v[js, :], src_part, NT)
            logit_v[js, :] = d
            return jnp.maximum(peak, jnp.max(d.reshape(block // 8, 8, width), axis=0))

        peak = lax.fori_loop(0, n_blocks, products, jnp.full((8, width), -3.0e38, jnp.float32))
        peak = jnp.max(peak, axis=0, keepdims=True)

        def exponentials(b, total):
            js = pl.ds(pl.multiple_of(b * block, block), block)
            e = jnp.exp2((logit_v[js, :] - peak) * SCALE)
            kt_v[js, lanes] = e.astype(jnp.bfloat16)
            return total + jnp.sum(e.reshape(block // 8, 8, width), axis=0)

        total = lax.fori_loop(0, n_blocks, exponentials, jnp.zeros((8, width), jnp.float32))
        total = jnp.sum(total, axis=0, keepdims=True)
        for h in range(width // LANES):
            t = i * (width // LANES) + h
            r1_send[t:t + 1, :] = peak[:, h * LANES:(h + 1) * LANES]
            r1_send[row_tiles + t:row_tiles + t + 1, :] = total[:, h * LANES:(h + 1) * LANES]

    pl.semaphore_wait(barrier, len(tgt_peers) + len(src_peers))
    start(r1_send, r1_recv, 0, tgt_peers)

    other_mass = jnp.exp(other_ref[...])
    src_counts = src_counts_ref[...].astype(jnp.float32)
    tgt_counts = tgt_counts_ref[...].astype(jnp.float32)
    row_lhs[...] = jnp.zeros_like(row_lhs)
    col_lhs[...] = jnp.zeros_like(col_lhs)
    loads[2].wait()

    def turn(b, carry):
        js = pl.ds(pl.multiple_of(b * 256, 256), 256)
        qt_v[:, js] = qwen_v[js, :].T
        return carry

    lax.fori_loop(0, cols // 256, turn, 0)

    def spread(lhs, dense, tiles):
        high = dense.astype(jnp.bfloat16).astype(jnp.float32)
        low = dense - high
        for t in range(tiles):
            lhs[0:1, t * LANES:(t + 1) * LANES] = high[t:t + 1, :]
            lhs[1:2, t * LANES:(t + 1) * LANES] = low[t:t + 1, :]

    def column_sums(dest):
        a = row_lhs[...].astype(jnp.bfloat16)

        for b in range(cols // 256):
            c = jnp.sum(dot(a, kt_v[b * 256:(b + 1) * 256, :], NT), axis=0, keepdims=True)
            for h in range(2):
                dest[2 * b + h:2 * b + h + 1, :] = c[:, h * LANES:(h + 1) * LANES]

    def row_sums():
        def body(b, acc):
            js = pl.ds(pl.multiple_of(b * 256, 256), 256)
            return acc + dot(col_lhs[:, js].astype(jnp.bfloat16), kt_v[js, :], NN)

        acc = lax.fori_loop(0, cols // 256, body, jnp.zeros((8, rows), jnp.float32))
        return jnp.sum(acc, axis=0, keepdims=True)

    wait_recv(r1_recv, 0)
    local_peak, local_total = r1_send[0:row_tiles, :], r1_send[row_tiles:2 * row_tiles, :]
    top = jnp.maximum(local_peak, jnp.max(r1_recv[:, 0:row_tiles, :], axis=0))
    factor = jnp.exp2((local_peak - top) * SCALE)
    mass = local_total * factor
    for d in range(n_tgt - 1):
        mass += r1_recv[d, row_tiles:2 * row_tiles, :] * jnp.exp2(
            (r1_recv[d, 0:row_tiles, :] - top) * SCALE
        )
    spread(row_lhs, src_counts / mass * factor, row_tiles)

    column_sums(c1_send)
    c1_send[col_tiles:, :] = jnp.full((2, LANES), jnp.sum(src_counts), jnp.float32)
    start(c1_send, c1_recv, 1, src_peers)
    r2_send[row_tiles:, :] = jnp.full((row_tiles, LANES), jnp.sum(tgt_counts), jnp.float32)
    wait_recv(c1_recv, 1)
    sums = c1_send[...] + jnp.sum(c1_recv[...], axis=0)
    slab_total = sums[col_tiles:col_tiles + 1, :]
    spread(col_lhs, tgt_counts / (sums[:col_tiles, :] / slab_total + other_mass), col_tiles)

    r = row_sums()
    for t in range(row_tiles):
        r2_send[t:t + 1, :] = r[:, t * LANES:(t + 1) * LANES] * factor[t:t + 1, :]
    start(r2_send, r2_recv, 2, tgt_peers)
    wait_recv(r2_recv, 2)
    sums = r2_send[...] + jnp.sum(r2_recv[...], axis=0)
    vocab_total = sums[row_tiles:, :]
    gain = factor / sums[:row_tiles, :]
    spread(row_lhs, src_counts / slab_total * vocab_total * gain, row_tiles)

    column_sums(c2_send)
    c2_send[col_tiles:, :] = jnp.zeros((2, LANES), jnp.float32)
    start(c2_send, c2_recv, 3, src_peers)
    wait_recv(c2_recv, 3)
    sums = c2_send[...] + jnp.sum(c2_recv[...], axis=0)
    spread(col_lhs, tgt_counts / (sums[:col_tiles, :] + other_mass), col_tiles)

    def weigh(b, carry):
        js = pl.ds(pl.multiple_of(b * 256, 256), 256)
        v = col_lhs[0:1, js] + col_lhs[1:2, js]
        qt_v[:, js] = (qt_v[:, js].astype(jnp.float32) * v).astype(jnp.bfloat16)
        return carry

    lax.fori_loop(0, cols // 256, weigh, 0)
    for i in range(rows // width):
        part = dot(qt_v[...], kt_v[:, i * width:(i + 1) * width], NN)
        for h in range(width // LANES):
            t = i * (width // LANES) + h
            turned = (part[:, h * LANES:(h + 1) * LANES] * gain[t:t + 1, :]).T
            f_send[t, :, :, :] = turned.reshape(NX, owned, turned.shape[1])

    for d in range(1, NX):
        peer_x = (me_x + d) % NX
        pltpu.make_async_remote_copy(
            src_ref=f_send.at[:, peer_x], dst_ref=f_recv.at[d - 1],
            send_sem=send_sem.at[4], recv_sem=recv_sem.at[4],
            device_id=(me_src, me_z * NX + peer_x), device_id_type=MESH,
        ).start()
    wait_recv(f_recv, 4)
    g_send[...] = f_send[:, me_x] + f_recv[0] + f_recv[1] + f_recv[2]
    for d in range(1, n_z):
        peer_z = (me_z + d) % n_z
        pltpu.make_async_remote_copy(
            src_ref=g_send.at[peer_z], dst_ref=g_recv.at[d - 1],
            send_sem=send_sem.at[5], recv_sem=recv_sem.at[5],
            device_id=(me_src, peer_z * NX + me_x), device_id_type=MESH,
        ).start()
    wait_recv(g_recv, 5)
    out_ref[...] = g_send[me_z] + jnp.sum(g_recv[...], axis=0)

    for k, recv_ref in enumerate((r1_recv, c1_recv, r2_recv, c2_recv, f_recv, g_recv)):
        wait_send(recv_ref, k)


def on_device(n_src, n_tgt, src_embed, tgt_embed, qwen_embed, other_log, src_counts, tgt_counts):
    rows, emb = src_embed.shape
    cols, dim = qwen_embed.shape
    row_tiles, col_tiles = rows // LANES, cols // LANES
    owned, n_z = rows // n_tgt, n_tgt // NX
    assert owned * NX == LANES
    f32, bf16 = jnp.float32, jnp.bfloat16
    vmem = pl.BlockSpec(memory_space=pltpu.VMEM)
    hbm = pl.BlockSpec(memory_space=pl.ANY)
    return pl.pallas_call(
        functools.partial(kernel, n_src, n_tgt),
        out_shape=jax.ShapeDtypeStruct((owned, dim), f32),
        in_specs=[hbm, hbm, hbm, vmem, vmem, vmem],
        out_specs=vmem,
        scratch_shapes=[
            pltpu.VMEM((rows, emb), bf16),
            pltpu.VMEM((cols, emb), bf16),
            pltpu.VMEM((cols, dim), bf16),
            pltpu.VMEM((dim, cols), bf16),
            pltpu.VMEM((cols, 256), f32),
            pltpu.VMEM((cols, rows), bf16),
            pltpu.VMEM((8, rows), f32),
            pltpu.VMEM((8, cols), f32),
            pltpu.VMEM((2 * row_tiles, LANES), f32),
            pltpu.VMEM((n_tgt - 1, 2 * row_tiles, LANES), f32),
            pltpu.VMEM((col_tiles + 2, LANES), f32),
            pltpu.VMEM((n_src - 1, col_tiles + 2, LANES), f32),
            pltpu.VMEM((2 * row_tiles, LANES), f32),
            pltpu.VMEM((n_tgt - 1, 2 * row_tiles, LANES), f32),
            pltpu.VMEM((col_tiles + 2, LANES), f32),
            pltpu.VMEM((n_src - 1, col_tiles + 2, LANES), f32),
            pltpu.VMEM((n_z, NX, owned, dim), f32),
            pltpu.VMEM((NX - 1, n_z, owned, dim), f32),
            pltpu.VMEM((n_z, owned, dim), f32),
            pltpu.VMEM((n_z - 1, owned, dim), f32),
            pltpu.SemaphoreType.DMA((3,)),
            pltpu.SemaphoreType.DMA((6,)),
            pltpu.SemaphoreType.DMA((6,)),
        ],
        compiler_params=pltpu.CompilerParams(
            collective_id=0, has_side_effects=True, vmem_limit_bytes=56 * 1024 * 1024
        ),
    )(
        src_embed, tgt_embed, qwen_embed,
        other_log.reshape(col_tiles, LANES),
        src_counts.reshape(row_tiles, LANES),
        tgt_counts.reshape(col_tiles, LANES),
    )


def solution(mesh):
    return jax.shard_map(
        functools.partial(on_device, mesh.shape["src"], mesh.shape["tgt"]),
        mesh=mesh,
        in_specs=(P("src", None), P("tgt", None), P("tgt", None), P("tgt"), P("src"), P("tgt")),
        out_specs=P(("src", "tgt"), None),
        check_vma=False,
    )
```

```python
import functools
import math

import jax
import jax.numpy as jnp
from jax import lax
from jax.experimental import pallas as pl
from jax.experimental.pallas import tpu as pltpu
from jax.sharding import PartitionSpec as P

MESH = pl.DeviceIdType.MESH
LANES = 128
WIDTH = 256
NX = 4
INV_TEMP = 4.0
SCALE = INV_TEMP * math.log2(math.e)
NT = (((1,), (1,)), ((), ()))
NN = (((1,), (0,)), ((), ()))


def dot(a, b, dims):
    return lax.dot_general(a, b, dims, preferred_element_type=jnp.float32)


def hops(d, n):
    return min(d, n - d)


def kernel(
    n_src, n_tgt,
    src_hbm, tgt_hbm, qwen_hbm, other_ref, src_counts_ref, tgt_counts_ref,
    out_ref,
    src_v, tgt_v, qwen_v, qt_v, logit_a, logit_b, kt_v, row_lhs, col_lhs, peak_v, gain_v,
    r1_send, r1_recv, t_send, t_recv, c1_send, c1_recv, r2_send, r2_recv, c2_send, c2_recv,
    f_send, hop_recv, relay_send, f_recv, g_send, g_recv,
    load_sem, send_sem, recv_sem, hop_sem, f_sem,
):
    rows = src_v.shape[0]
    cols = tgt_v.shape[0]
    n_z = n_tgt // NX
    row_tiles, col_tiles = rows // LANES, cols // LANES
    n_parts = rows // WIDTH
    me_src, me_tgt = lax.axis_index("src"), lax.axis_index("tgt")
    me_z, me_x = me_tgt // NX, me_tgt % NX

    n_blocks = 4
    block = cols // n_blocks
    step = block // 4

    def load_tgt(b):
        js = pl.ds(b * block, block)
        return pltpu.make_async_copy(tgt_hbm.at[js, :], tgt_v.at[js, :], load_sem.at[2 + b])

    load_src = pltpu.make_async_copy(src_hbm, src_v, load_sem.at[0])
    load_qwen = pltpu.make_async_copy(qwen_hbm, qwen_v, load_sem.at[1])
    load_src.start()
    for b in range(n_blocks):
        load_tgt(b).start()
    load_qwen.start()

    far = sorted(range(1, n_tgt), key=lambda d: -hops(d // NX, n_z) - hops(d % NX, NX))
    tgt_peers = [(me_src, (me_tgt + d) % n_tgt) for d in far]
    src_peers = [
        ((me_src + d) % n_src, me_tgt)
        for d in sorted(range(1, n_src), key=lambda d: -hops(d, n_src))
    ]
    barrier = pltpu.get_barrier_semaphore()
    for peer in tgt_peers + src_peers:
        pl.semaphore_signal(barrier, inc=1, device_id=peer, device_id_type=MESH)

    def send(src, dst, k, sem, peer):
        pltpu.make_async_remote_copy(
            src_ref=src, dst_ref=dst, send_sem=send_sem.at[k], recv_sem=sem,
            device_id=peer, device_id_type=MESH,
        ).start()

    def start(send_ref, recv_ref, k, peers):
        for slot, peer in enumerate(peers):
            send(send_ref, recv_ref.at[slot], k, recv_sem.at[k], peer)

    def wait(ref, sem):
        pltpu.make_async_copy(ref, ref, sem).wait()

    load_src.wait()

    def products(logit, i, js, peak):
        d = dot(tgt_v[js, :], src_v[i * WIDTH:(i + 1) * WIDTH, :], NT)
        logit[js, :] = d
        return jnp.maximum(peak, jnp.max(d.reshape(step // 8, 8, WIDTH), axis=0))

    def exponentials(logit, i, js, peak, total):
        e = jnp.exp2((logit[js, :] - peak) * SCALE)
        kt_v[js, i * WIDTH:(i + 1) * WIDTH] = e.astype(jnp.bfloat16)
        return total + jnp.sum(e.reshape(step // 8, 8, WIDTH), axis=0)

    def steps(b):
        for s in range(block // step):
            yield pl.ds(pl.multiple_of(b * block + s * step, step), step)

    low = jnp.full((8, WIDTH), -3.0e38, jnp.float32)
    zero = jnp.zeros((8, WIDTH), jnp.float32)
    logits = (logit_a, logit_b)

    def first(b, peak):
        load_tgt(b).wait()
        for js in steps(b):
            peak = products(logits[0], 0, js, peak)
        return peak

    peak = lax.fori_loop(0, n_blocks, first, low)
    for i in range(n_parts):
        peak = jnp.max(peak, axis=0, keepdims=True)

        def both(b, carry, peak=peak, i=i):
            later, total = carry
            for js in steps(b):
                if i + 1 < n_parts:
                    later = products(logits[(i + 1) % 2], i + 1, js, later)
                total = exponentials(logits[i % 2], i, js, peak, total)
            return later, total

        later, total = lax.fori_loop(0, n_blocks, both, (low, zero))
        lse = INV_TEMP * peak + jnp.log(jnp.sum(total, axis=0, keepdims=True))
        for h in range(WIDTH // LANES):
            t = i * (WIDTH // LANES) + h
            peak_v[t:t + 1, :] = peak[:, h * LANES:(h + 1) * LANES]
            r1_send[t:t + 1, :] = lse[:, h * LANES:(h + 1) * LANES]
        peak = later

    pl.semaphore_wait(barrier, len(tgt_peers) + len(src_peers))
    start(r1_send, r1_recv, 0, tgt_peers)

    tgt_counts = tgt_counts_ref[...].astype(jnp.float32)
    t_send[...] = jnp.full((1, LANES), jnp.sum(tgt_counts), jnp.float32)
    start(t_send, t_recv, 1, tgt_peers)
    other_mass = jnp.exp(other_ref[...])
    src_counts = src_counts_ref[...].astype(jnp.float32)
    row_lhs[...] = jnp.zeros_like(row_lhs)
    col_lhs[...] = jnp.zeros_like(col_lhs)
    c1_send[col_tiles:, :] = jnp.full((2, LANES), jnp.sum(src_counts), jnp.float32)
    load_qwen.wait()

    def turn(b, carry):
        js = pl.ds(pl.multiple_of(b * 256, 256), 256)
        qt_v[:, js] = qwen_v[js, :].T
        return carry

    lax.fori_loop(0, cols // 256, turn, 0)

    def spread(lhs, dense, tiles):
        high = dense.astype(jnp.bfloat16).astype(jnp.float32)
        rest = dense - high
        for t in range(tiles):
            lhs[0:1, t * LANES:(t + 1) * LANES] = high[t:t + 1, :]
            lhs[1:2, t * LANES:(t + 1) * LANES] = rest[t:t + 1, :]

    def column_sums(dest):
        a = row_lhs[...].astype(jnp.bfloat16)
        for b in range(cols // 256):
            c = jnp.sum(dot(a, kt_v[b * 256:(b + 1) * 256, :], NT), axis=0, keepdims=True)
            for h in range(2):
                dest[2 * b + h:2 * b + h + 1, :] = c[:, h * LANES:(h + 1) * LANES]

    wait(r1_recv, recv_sem.at[0])
    top = jnp.maximum(r1_send[...], jnp.max(r1_recv[...], axis=0))
    mass = jnp.exp(r1_send[...] - top) + jnp.sum(jnp.exp(r1_recv[...] - top), axis=0)
    factor = jnp.exp(INV_TEMP * peak_v[...] - (top + jnp.log(mass)))
    spread(row_lhs, src_counts * factor, row_tiles)

    column_sums(c1_send)
    start(c1_send, c1_recv, 2, src_peers)
    wait(t_recv, recv_sem.at[1])
    vocab_total = t_send[...] + jnp.sum(t_recv[...], axis=0)
    wait(c1_recv, recv_sem.at[2])
    sums = c1_send[...] + jnp.sum(c1_recv[...], axis=0)
    slab_total = sums[col_tiles:col_tiles + 1, :]
    spread(col_lhs, tgt_counts / (sums[:col_tiles, :] / slab_total + other_mass), col_tiles)

    r = jnp.sum(dot(col_lhs[...].astype(jnp.bfloat16), kt_v[...], NN), axis=0, keepdims=True)
    for t in range(row_tiles):
        r2_send[t:t + 1, :] = r[:, t * LANES:(t + 1) * LANES] * factor[t:t + 1, :]
    start(r2_send, r2_recv, 3, tgt_peers)
    wait(r2_recv, recv_sem.at[3])
    gain = factor / (r2_send[...] + jnp.sum(r2_recv[...], axis=0))
    gain_v[...] = gain
    spread(row_lhs, src_counts / slab_total * vocab_total * gain, row_tiles)

    column_sums(c2_send)
    start(c2_send, c2_recv, 4, src_peers)
    wait(c2_recv, recv_sem.at[4])
    sums = c2_send[...] + jnp.sum(c2_recv[...], axis=0)
    spread(col_lhs, tgt_counts / (sums + other_mass), col_tiles)

    for b in range(n_blocks):
        js = slice(b * block, (b + 1) * block)
        v = col_lhs[0:1, js] + col_lhs[1:2, js]
        qt_v[:, js] = (qt_v[:, js].astype(jnp.float32) * v).astype(jnp.bfloat16)

    right, left, across = (me_x + 1) % NX, (me_x + NX - 1) % NX, (me_x + 2) % NX
    to_right, to_left = (me_src, me_z * NX + right), (me_src, me_z * NX + left)
    order = sorted(range(n_parts), key=lambda k: -hops(k, n_parts))
    pair_of = [(me_z // 2 + d) % n_parts for d in order]

    def transport(k):
        lanes = pl.ds(pl.multiple_of(pair_of[k] * WIDTH, WIDTH), WIDTH)
        part = dot(qt_v[...], kt_v[:, lanes], NN)
        for h in range(2):
            scale = gain_v[pl.ds(pair_of[k] * 2 + h, 1), :]
            turned = (part[:, h * LANES:(h + 1) * LANES] * scale).T
            f_send[k, h] = turned.reshape(f_send.shape[2:])
        send(f_send.at[k, 0, across], hop_recv.at[k, 0], 5, hop_sem.at[k], to_right)
        send(f_send.at[k, 1, across], hop_recv.at[k, 1], 5, hop_sem.at[k], to_left)
        send(f_send.at[k, 1, right], f_recv.at[k, 0], 6, f_sem.at[k], to_right)
        send(f_send.at[k, 0, left], f_recv.at[k, 1], 6, f_sem.at[k], to_left)

    def relay(k):
        wait(hop_recv.at[k], hop_sem.at[k])
        relay_send[k, 0] = f_send[k, 0, right] + hop_recv[k, 0]
        relay_send[k, 1] = f_send[k, 1, left] + hop_recv[k, 1]
        send(relay_send.at[k, 0], f_recv.at[k, 2], 6, f_sem.at[k], to_right)
        send(relay_send.at[k, 1], f_recv.at[k, 3], 6, f_sem.at[k], to_left)

    def gather(k):
        wait(f_recv.at[k], f_sem.at[k])
        g_send[k, 0] = f_send[k, 0, me_x] + f_recv[k, 1] + f_recv[k, 2]
        g_send[k, 1] = f_send[k, 1, me_x] + f_recv[k, 0] + f_recv[k, 3]
        for h in range(2) if k < n_parts - 1 else [1 - me_z % 2]:
            z = pair_of[k] * 2 + h
            slot = (z - me_z + n_z) % n_z - 1
            send(g_send.at[k, h], g_recv.at[slot], 7, recv_sem.at[5], (me_src, z * NX + me_x))

    for k in range(n_parts + 2):
        if k < n_parts:
            transport(k)
        if 1 <= k <= n_parts:
            relay(k - 1)
        if k >= 2:
            gather(k - 2)

    wait(g_recv, recv_sem.at[5])
    out_ref[...] = g_send[n_parts - 1, me_z % 2] + jnp.sum(g_recv[...], axis=0)

    sent = (r1_recv, t_recv, c1_recv, r2_recv, c2_recv, hop_recv, f_recv, g_recv)
    for k, ref in enumerate(sent):
        wait(ref, send_sem.at[k])


def on_device(n_src, n_tgt, src_embed, tgt_embed, qwen_embed, other_log, src_counts, tgt_counts):
    rows, emb = src_embed.shape
    cols, dim = qwen_embed.shape
    row_tiles, col_tiles = rows // LANES, cols // LANES
    owned, n_z, n_parts = rows // n_tgt, n_tgt // NX, rows // WIDTH
    assert owned * NX == LANES and n_parts * 2 == n_z
    f32, bf16 = jnp.float32, jnp.bfloat16
    vmem = pl.BlockSpec(memory_space=pltpu.VMEM)
    hbm = pl.BlockSpec(memory_space=pl.ANY)
    return pl.pallas_call(
        functools.partial(kernel, n_src, n_tgt),
        out_shape=jax.ShapeDtypeStruct((owned, dim), f32),
        in_specs=[hbm, hbm, hbm, vmem, vmem, vmem],
        out_specs=vmem,
        scratch_shapes=[
            pltpu.VMEM((rows, emb), bf16),
            pltpu.VMEM((cols, emb), bf16),
            pltpu.VMEM((cols, dim), bf16),
            pltpu.VMEM((dim, cols), bf16),
            pltpu.VMEM((cols, WIDTH), f32),
            pltpu.VMEM((cols, WIDTH), f32),
            pltpu.VMEM((cols, rows), bf16),
            pltpu.VMEM((8, rows), f32),
            pltpu.VMEM((8, cols), f32),
            pltpu.VMEM((row_tiles, LANES), f32),
            pltpu.VMEM((row_tiles, LANES), f32),
            pltpu.VMEM((row_tiles, LANES), f32),
            pltpu.VMEM((n_tgt - 1, row_tiles, LANES), f32),
            pltpu.VMEM((1, LANES), f32),
            pltpu.VMEM((n_tgt - 1, 1, LANES), f32),
            pltpu.VMEM((col_tiles + 2, LANES), f32),
            pltpu.VMEM((n_src - 1, col_tiles + 2, LANES), f32),
            pltpu.VMEM((row_tiles, LANES), f32),
            pltpu.VMEM((n_tgt - 1, row_tiles, LANES), f32),
            pltpu.VMEM((col_tiles, LANES), f32),
            pltpu.VMEM((n_src - 1, col_tiles, LANES), f32),
            pltpu.VMEM((n_parts, 2, NX, owned, dim), f32),
            pltpu.VMEM((n_parts, 2, owned, dim), f32),
            pltpu.VMEM((n_parts, 2, owned, dim), f32),
            pltpu.VMEM((n_parts, 4, owned, dim), f32),
            pltpu.VMEM((n_parts, 2, owned, dim), f32),
            pltpu.VMEM((n_z - 1, owned, dim), f32),
            pltpu.SemaphoreType.DMA((6,)),
            pltpu.SemaphoreType.DMA((8,)),
            pltpu.SemaphoreType.DMA((6,)),
            pltpu.SemaphoreType.DMA((n_parts,)),
            pltpu.SemaphoreType.DMA((n_parts,)),
        ],
        compiler_params=pltpu.CompilerParams(
            collective_id=0, has_side_effects=True, vmem_limit_bytes=56 * 1024 * 1024
        ),
    )(
        src_embed, tgt_embed, qwen_embed,
        other_log.reshape(col_tiles, LANES),
        src_counts.reshape(row_tiles, LANES),
        tgt_counts.reshape(col_tiles, LANES),
    )


def solution(mesh):
    return jax.shard_map(
        functools.partial(on_device, mesh.shape["src"], mesh.shape["tgt"]),
        mesh=mesh,
        in_specs=(P("src", None), P("tgt", None), P("tgt", None), P("tgt"), P("src"), P("tgt")),
        out_specs=P(("src", "tgt"), None),
        check_vma=False,
    )
```

```python
import functools
import math

import jax
import jax.numpy as jnp
from jax import lax
from jax.experimental import pallas as pl
from jax.experimental.pallas import tpu as pltpu
from jax.sharding import PartitionSpec as P

MESH = pl.DeviceIdType.MESH
LANES = 128
WIDTH = 256
NX = 4
INV_TEMP = 4.0
SCALE = INV_TEMP * math.log2(math.e)
NT = (((1,), (1,)), ((), ()))
NN = (((1,), (0,)), ((), ()))


def dot(a, b, dims):
    return lax.dot_general(a, b, dims, preferred_element_type=jnp.float32)


def hops(d, n):
    return min(d, n - d)


def kernel(
    n_src, n_tgt,
    src_hbm, tgt_hbm, qwen_hbm, other_hbm, src_counts_hbm, tgt_counts_hbm,
    out_ref,
    other_ref, src_counts_ref, tgt_counts_ref, src_v, tgt_v, qwen_v, qt_v, logit_a, logit_b, kt_v, row_lhs, col_lhs, peak_v, gain_v,
    r1_send, r1_recv, t_send, t_recv, c1_send, c1_recv, r2_send, r2_recv, c2_send, c2_recv,
    f_send, f_recv, g_send, g_recv, d_recv,
    load_sem, send_sem, recv_sem, f_sem,
):
    rows = src_v.shape[0]
    cols = tgt_v.shape[0]
    n_z = n_tgt // NX
    row_tiles, col_tiles = rows // LANES, cols // LANES
    n_parts = rows // WIDTH
    width = logit_a.shape[1]
    n_wide = rows // width
    me_src, me_tgt = lax.axis_index("src"), lax.axis_index("tgt")
    me_z, me_x = me_tgt // NX, me_tgt % NX

    n_blocks = 4
    block = cols // n_blocks
    step = block // 4
    wide = cols // 4

    def load_tgt(b):
        js = pl.ds(b * block, block)
        return pltpu.make_async_copy(tgt_hbm.at[js, :], tgt_v.at[js, :], load_sem.at[2 + b])

    load_src = pltpu.make_async_copy(src_hbm, src_v, load_sem.at[0])
    load_qwen = pltpu.make_async_copy(qwen_hbm, qwen_v, load_sem.at[1])
    load_src.start()
    for b in range(n_blocks):
        load_tgt(b).start()
    load_qwen.start()
    load_small = [
        pltpu.make_async_copy(src_counts_hbm, src_counts_ref, load_sem.at[6]),
        pltpu.make_async_copy(tgt_counts_hbm, tgt_counts_ref, load_sem.at[7]),
        pltpu.make_async_copy(other_hbm, other_ref, load_sem.at[8]),
    ]
    for load in load_small:
        load.start()

    far = sorted(range(1, n_tgt), key=lambda d: -hops(d // NX, n_z) - hops(d % NX, NX))
    tgt_peers = [(me_src, (me_tgt + d) % n_tgt) for d in far]
    src_peers = [
        ((me_src + d) % n_src, me_tgt)
        for d in sorted(range(1, n_src), key=lambda d: -hops(d, n_src))
    ]
    barrier = pltpu.get_barrier_semaphore()
    for peer in tgt_peers + src_peers:
        pl.semaphore_signal(barrier, inc=1, device_id=peer, device_id_type=MESH)

    def send(src, dst, k, sem, peer):
        pltpu.make_async_remote_copy(
            src_ref=src, dst_ref=dst, send_sem=send_sem.at[k], recv_sem=sem,
            device_id=peer, device_id_type=MESH,
        ).start()

    def start(send_ref, recv_ref, k, peers):
        for slot, peer in enumerate(peers):
            send(send_ref, recv_ref.at[slot], k, recv_sem.at[k], peer)

    def wait(ref, sem):
        pltpu.make_async_copy(ref, ref, sem).wait()

    load_src.wait()

    def products(logit, i, js, peak):
        d = dot(tgt_v[js, :], src_v[i * width:(i + 1) * width, :], NT)
        logit[js, :] = d
        return jnp.maximum(peak, jnp.max(d.reshape(step // 8, 8, width), axis=0))

    def exponentials(logit, i, js, peak, total):
        e = jnp.exp2((logit[js, :] - peak) * SCALE)
        kt_v[js, i * width:(i + 1) * width] = e.astype(jnp.bfloat16)
        return total + jnp.sum(e.reshape(step // 8, 8, width), axis=0)

    def steps(b, size):
        for s in range(size // step):
            yield pl.ds(pl.multiple_of(b * size + s * step, step), step)

    low = jnp.full((8, width), -3.0e38, jnp.float32)
    zero = jnp.zeros((8, width), jnp.float32)
    logits = (logit_a, logit_b)

    def first(b, peak):
        load_tgt(b).wait()
        for js in steps(b, block):
            peak = products(logits[0], 0, js, peak)
        return peak

    peak = lax.fori_loop(0, n_blocks, first, low)
    for i in range(n_wide):
        peak = jnp.max(peak, axis=0, keepdims=True)

        def both(b, carry, peak=peak, i=i):
            later, total = carry
            for js in steps(b, wide):
                if i + 1 < n_wide:
                    later = products(logits[(i + 1) % 2], i + 1, js, later)
                total = exponentials(logits[i % 2], i, js, peak, total)
            return later, total

        later, total = lax.fori_loop(0, 4, both, (low, zero))
        lse = INV_TEMP * peak + jnp.log(jnp.sum(total, axis=0, keepdims=True))
        for h in range(width // LANES):
            t = i * (width // LANES) + h
            peak_v[t:t + 1, :] = peak[:, h * LANES:(h + 1) * LANES]
            r1_send[t:t + 1, :] = lse[:, h * LANES:(h + 1) * LANES]
        peak = later

    pl.semaphore_wait(barrier, len(tgt_peers) + len(src_peers))
    start(r1_send, r1_recv, 0, tgt_peers)

    for load in load_small:
        load.wait()
    tgt_counts = tgt_counts_ref[...].astype(jnp.float32)
    t_send[...] = jnp.full((1, LANES), jnp.sum(tgt_counts), jnp.float32)
    start(t_send, t_recv, 1, tgt_peers)
    other_mass = jnp.exp(other_ref[...])
    src_counts = src_counts_ref[...].astype(jnp.float32)
    row_lhs[...] = jnp.zeros_like(row_lhs)
    col_lhs[...] = jnp.zeros_like(col_lhs)
    c1_send[col_tiles:, :] = jnp.full((2, LANES), jnp.sum(src_counts), jnp.float32)
    load_qwen.wait()

    def turn(b, carry):
        js = pl.ds(pl.multiple_of(b * 256, 256), 256)
        qt_v[:, js] = qwen_v[js, :].T
        return carry

    lax.fori_loop(0, cols // 256, turn, 0)

    def spread(lhs, dense, tiles):
        high = dense.astype(jnp.bfloat16).astype(jnp.float32)
        rest = dense - high
        for t in range(tiles):
            lhs[0:1, t * LANES:(t + 1) * LANES] = high[t:t + 1, :]
            lhs[1:2, t * LANES:(t + 1) * LANES] = rest[t:t + 1, :]

    half = col_tiles // 16 * 8

    def column_exchange(dest, recv_ref, k):
        a = row_lhs[...].astype(jnp.bfloat16)
        for b in range(cols // 256):
            c = jnp.sum(dot(a, kt_v[b * 256:(b + 1) * 256, :], NT), axis=0, keepdims=True)
            for h in range(2):
                dest[2 * b + h:2 * b + h + 1, :] = c[:, h * LANES:(h + 1) * LANES]
            if 2 * (b + 1) == half:
                part = pl.ds(0, half)
                start(dest.at[part], recv_ref.at[:, part], k, src_peers)
        part = pl.ds(half, dest.shape[0] - half)
        start(dest.at[part], recv_ref.at[:, part], k, src_peers)

    wait(r1_recv, recv_sem.at[0])
    top = jnp.maximum(r1_send[...], jnp.max(r1_recv[...], axis=0))
    mass = jnp.exp(r1_send[...] - top) + jnp.sum(jnp.exp(r1_recv[...] - top), axis=0)
    factor = jnp.exp(INV_TEMP * peak_v[...] - (top + jnp.log(mass)))
    spread(row_lhs, src_counts * factor, row_tiles)

    column_exchange(c1_send, c1_recv, 2)
    wait(t_recv, recv_sem.at[1])
    vocab_total = t_send[...] + jnp.sum(t_recv[...], axis=0)
    wait(c1_recv, recv_sem.at[2])
    sums = c1_send[...] + jnp.sum(c1_recv[...], axis=0)
    slab_total = sums[col_tiles:col_tiles + 1, :]
    spread(col_lhs, tgt_counts / (sums[:col_tiles, :] / slab_total + other_mass), col_tiles)

    r = jnp.sum(dot(col_lhs[...].astype(jnp.bfloat16), kt_v[...], NN), axis=0, keepdims=True)
    for t in range(row_tiles):
        r2_send[t:t + 1, :] = r[:, t * LANES:(t + 1) * LANES] * factor[t:t + 1, :]
    start(r2_send, r2_recv, 3, tgt_peers)
    wait(r2_recv, recv_sem.at[3])
    gain = factor / (r2_send[...] + jnp.sum(r2_recv[...], axis=0))
    gain_v[...] = gain
    spread(row_lhs, src_counts / slab_total * vocab_total * gain, row_tiles)

    column_exchange(c2_send, c2_recv, 4)
    wait(c2_recv, recv_sem.at[4])
    sums = c2_send[...] + jnp.sum(c2_recv[...], axis=0)
    spread(col_lhs, tgt_counts / (sums + other_mass), col_tiles)

    for b in range(n_blocks):
        js = slice(b * block, (b + 1) * block)
        v = col_lhs[0:1, js] + col_lhs[1:2, js]
        qt_v[:, js] = (qt_v[:, js].astype(jnp.float32) * v).astype(jnp.bfloat16)

    order = sorted(range(n_parts), key=lambda k: -hops(k, n_parts))
    pair_of = [(me_z // 2 + d) % n_parts for d in order]
    n_first = f_recv.shape[0]
    side = me_z % 2
    xs = sorted(range(NX), key=lambda d: -hops(d, NX))

    def transport(k):
        lanes = pl.ds(pl.multiple_of(pair_of[k] * WIDTH, WIDTH), WIDTH)
        part = dot(qt_v[...], kt_v[:, lanes], NN)
        for h in range(2):
            scale = gain_v[pl.ds(pair_of[k] * 2 + h, 1), :]
            turned = (part[:, h * LANES:(h + 1) * LANES] * scale).T
            f_send[k, h] = turned.reshape(f_send.shape[2:])

    def over_x(k):
        for d in xs[:-1]:
            x = (me_x + d) % NX
            send(f_send.at[k, :, x], f_recv.at[k, d - 1], 5, f_sem.at[k], (me_src, me_z * NX + x))

    def over_z(k):
        wait(f_recv.at[k], f_sem.at[k])
        g_send[k] = f_send[k, :, me_x] + jnp.sum(f_recv[k], axis=0)
        for h in range(2):
            owner = (me_src, (pair_of[k] * 2 + h) * NX + me_x)
            send(g_send.at[k, h], g_recv.at[2 * k + side], 6, recv_sem.at[5], owner)

    def straight(k):
        for d in xs:
            x = (me_x + d) % NX
            for h in range(2):
                if h == 0 and d == 0:
                    continue
                half = (side + h) % 2
                owner = (me_src, (pair_of[k] * 2 + half) * NX + x)
                send(f_send.at[k, half, x], d_recv.at[h * NX + d - 1], 7, recv_sem.at[6], owner)

    for k in range(n_parts):
        transport(k)
        if k < n_first:
            over_x(k)
    for k in range(n_first):
        if k == n_first - 1:
            straight(n_parts - 1)
        over_z(k)

    wait(g_recv, recv_sem.at[5])
    wait(d_recv, recv_sem.at[6])
    total = f_send[n_parts - 1, side, me_x] + jnp.sum(d_recv[...], axis=0)
    out_ref[...] = total + jnp.sum(g_recv[...], axis=0)

    sent = (r1_recv, t_recv, c1_recv, r2_recv, c2_recv, f_recv, g_recv, d_recv)
    for k, ref in enumerate(sent):
        wait(ref, send_sem.at[k])


def on_device(n_src, n_tgt, src_embed, tgt_embed, qwen_embed, other_log, src_counts, tgt_counts):
    rows, emb = src_embed.shape
    cols, dim = qwen_embed.shape
    row_tiles, col_tiles = rows // LANES, cols // LANES
    owned, n_z, n_parts = rows // n_tgt, n_tgt // NX, rows // WIDTH
    assert owned * NX == LANES and n_parts * 2 == n_z
    n_first = n_parts - 1
    f32, bf16 = jnp.float32, jnp.bfloat16
    vmem = pl.BlockSpec(memory_space=pltpu.VMEM)
    hbm = pl.BlockSpec(memory_space=pltpu.HBM)
    return pl.pallas_call(
        functools.partial(kernel, n_src, n_tgt),
        out_shape=jax.ShapeDtypeStruct((owned, dim), f32),
        in_specs=[hbm] * 6,
        out_specs=vmem,
        scratch_shapes=[
            pltpu.VMEM((col_tiles, LANES), f32),
            pltpu.VMEM((row_tiles, LANES), jnp.int32),
            pltpu.VMEM((col_tiles, LANES), jnp.int32),
            pltpu.VMEM((rows, emb), bf16),
            pltpu.VMEM((cols, emb), bf16),
            pltpu.VMEM((cols, dim), bf16),
            pltpu.VMEM((dim, cols), bf16),
            pltpu.VMEM((cols, min(512, rows)), f32),
            pltpu.VMEM((cols, min(512, rows)), f32),
            pltpu.VMEM((cols, rows), bf16),
            pltpu.VMEM((8, rows), f32),
            pltpu.VMEM((8, cols), f32),
            pltpu.VMEM((row_tiles, LANES), f32),
            pltpu.VMEM((row_tiles, LANES), f32),
            pltpu.VMEM((row_tiles, LANES), f32),
            pltpu.VMEM((n_tgt - 1, row_tiles, LANES), f32),
            pltpu.VMEM((1, LANES), f32),
            pltpu.VMEM((n_tgt - 1, 1, LANES), f32),
            pltpu.VMEM((col_tiles + 2, LANES), f32),
            pltpu.VMEM((n_src - 1, col_tiles + 2, LANES), f32),
            pltpu.VMEM((row_tiles, LANES), f32),
            pltpu.VMEM((n_tgt - 1, row_tiles, LANES), f32),
            pltpu.VMEM((col_tiles, LANES), f32),
            pltpu.VMEM((n_src - 1, col_tiles, LANES), f32),
            pltpu.VMEM((n_parts, 2, NX, owned, dim), f32),
            pltpu.VMEM((n_first, NX - 1, 2, owned, dim), f32),
            pltpu.VMEM((n_first, 2, owned, dim), f32),
            pltpu.VMEM((2 * n_first, owned, dim), f32),
            pltpu.VMEM((2 * NX - 1, owned, dim), f32),
            pltpu.SemaphoreType.DMA((9,)),
            pltpu.SemaphoreType.DMA((8,)),
            pltpu.SemaphoreType.DMA((7,)),
            pltpu.SemaphoreType.DMA((n_first,)),
        ],
        compiler_params=pltpu.CompilerParams(
            collective_id=0, has_side_effects=True, vmem_limit_bytes=56 * 1024 * 1024
        ),
    )(
        src_embed, tgt_embed, qwen_embed,
        other_log.reshape(col_tiles, LANES),
        src_counts.reshape(row_tiles, LANES),
        tgt_counts.reshape(col_tiles, LANES),
    )


def solution(mesh):
    return jax.shard_map(
        functools.partial(on_device, mesh.shape["src"], mesh.shape["tgt"]),
        mesh=mesh,
        in_specs=(P("src", None), P("tgt", None), P("tgt", None), P("tgt"), P("src"), P("tgt")),
        out_specs=P(("src", "tgt"), None),
        check_vma=False,
    )
```

```python
import functools
import math

import jax
import jax.numpy as jnp
from jax import lax
from jax.experimental import pallas as pl
from jax.experimental.pallas import tpu as pltpu
from jax.sharding import PartitionSpec as P

MESH = pl.DeviceIdType.MESH
LANES = 128
WIDTH = 256
NX = 4
INV_TEMP = 4.0
SCALE = INV_TEMP * math.log2(math.e)
NT = (((1,), (1,)), ((), ()))
NN = (((1,), (0,)), ((), ()))


def dot(a, b, dims):
    return lax.dot_general(a, b, dims, preferred_element_type=jnp.float32)


def hops(d, n):
    return min(d, n - d)


def kernel(
    n_src, n_tgt,
    src_hbm, tgt_hbm, qwen_hbm, other_hbm, src_counts_hbm, tgt_counts_hbm,
    out_ref,
    other_ref, src_counts_ref, tgt_counts_ref, src_v, tgt_v, qwen_v, qt_v, logit_a, logit_b, kt_v, row_lhs, col_lhs, peak_v, gain_v,
    r1_send, r1_recv, t_send, t_recv, c1_send, c1_recv, r2_send, r2_recv, c2_send, c2_recv,
    f_send, f_recv, g_send, g_recv, d_recv,
    load_sem, send_sem, recv_sem, f_sem,
):
    rows = src_v.shape[0]
    cols = tgt_v.shape[0]
    n_z = n_tgt // NX
    row_tiles, col_tiles = rows // LANES, cols // LANES
    n_parts = rows // WIDTH
    width = logit_a.shape[1]
    n_wide = rows // width
    me_src, me_tgt = lax.axis_index("src"), lax.axis_index("tgt")
    me_z, me_x = me_tgt // NX, me_tgt % NX

    n_blocks = 4
    block = cols // n_blocks
    step = block // 4
    wide = cols // 4

    def load_tgt(b):
        js = pl.ds(b * block, block)
        return pltpu.make_async_copy(tgt_hbm.at[js, :], tgt_v.at[js, :], load_sem.at[2 + b])

    load_src = pltpu.make_async_copy(src_hbm, src_v, load_sem.at[0])
    load_qwen = pltpu.make_async_copy(qwen_hbm, qwen_v, load_sem.at[1])
    load_src.start()
    for b in range(n_blocks):
        load_tgt(b).start()
    load_small = [
        pltpu.make_async_copy(src_counts_hbm, src_counts_ref, load_sem.at[6]),
        pltpu.make_async_copy(tgt_counts_hbm, tgt_counts_ref, load_sem.at[7]),
        pltpu.make_async_copy(other_hbm, other_ref, load_sem.at[8]),
    ]
    for load in load_small:
        load.start()

    far = sorted(range(1, n_tgt), key=lambda d: -hops(d // NX, n_z) - hops(d % NX, NX))
    tgt_peers = [(me_src, (me_tgt + d) % n_tgt) for d in far]
    src_peers = [
        ((me_src + d) % n_src, me_tgt)
        for d in sorted(range(1, n_src), key=lambda d: -hops(d, n_src))
    ]
    barrier = pltpu.get_barrier_semaphore()
    for peer in tgt_peers + src_peers:
        pl.semaphore_signal(barrier, inc=1, device_id=peer, device_id_type=MESH)

    def send(src, dst, k, sem, peer):
        pltpu.make_async_remote_copy(
            src_ref=src, dst_ref=dst, send_sem=send_sem.at[k], recv_sem=sem,
            device_id=peer, device_id_type=MESH,
        ).start()

    def start(send_ref, recv_ref, k, peers):
        for slot, peer in enumerate(peers):
            send(send_ref, recv_ref.at[slot], k, recv_sem.at[k], peer)

    def wait(ref, sem):
        pltpu.make_async_copy(ref, ref, sem).wait()

    load_src.wait()

    def products(logit, i, js, peak):
        d = dot(tgt_v[js, :], src_v[i * width:(i + 1) * width, :], NT)
        logit[js, :] = d
        return jnp.maximum(peak, jnp.max(d.reshape(step // 8, 8, width), axis=0))

    def exponentials(logit, i, js, peak, total):
        e = jnp.exp2((logit[js, :] - peak) * SCALE)
        kt_v[js, i * width:(i + 1) * width] = e.astype(jnp.bfloat16)
        return total + jnp.sum(e.reshape(step // 8, 8, width), axis=0)

    def steps(b, size):
        for s in range(size // step):
            yield pl.ds(pl.multiple_of(b * size + s * step, step), step)

    low = jnp.full((8, width), -3.0e38, jnp.float32)
    zero = jnp.zeros((8, width), jnp.float32)
    logits = (logit_a, logit_b)

    def first(b, peak):
        load_tgt(b).wait()
        for js in steps(b, block):
            peak = products(logits[0], 0, js, peak)
        return peak

    peak = lax.fori_loop(0, n_blocks, first, low)
    load_qwen.start()
    for i in range(n_wide):
        peak = jnp.max(peak, axis=0, keepdims=True)

        def both(b, carry, peak=peak, i=i):
            later, total = carry
            for js in steps(b, wide):
                if i + 1 < n_wide:
                    later = products(logits[(i + 1) % 2], i + 1, js, later)
                total = exponentials(logits[i % 2], i, js, peak, total)
            return later, total

        later, total = lax.fori_loop(0, 4, both, (low, zero))
        lse = INV_TEMP * peak + jnp.log(jnp.sum(total, axis=0, keepdims=True))
        for h in range(width // LANES):
            t = i * (width // LANES) + h
            peak_v[t:t + 1, :] = peak[:, h * LANES:(h + 1) * LANES]
            r1_send[t:t + 1, :] = lse[:, h * LANES:(h + 1) * LANES]
        peak = later

    pl.semaphore_wait(barrier, len(tgt_peers) + len(src_peers))
    start(r1_send, r1_recv, 0, tgt_peers)

    for load in load_small:
        load.wait()
    tgt_counts = tgt_counts_ref[...].astype(jnp.float32)
    t_send[...] = jnp.full((1, LANES), jnp.sum(tgt_counts), jnp.float32)
    start(t_send, t_recv, 1, tgt_peers)
    other_mass = jnp.exp(other_ref[...])
    src_counts = src_counts_ref[...].astype(jnp.float32)
    row_lhs[...] = jnp.zeros_like(row_lhs)
    col_lhs[...] = jnp.zeros_like(col_lhs)
    c1_send[col_tiles:, :] = jnp.full((2, LANES), jnp.sum(src_counts), jnp.float32)
    load_qwen.wait()

    def turn(b, carry):
        js = pl.ds(pl.multiple_of(b * 256, 256), 256)
        qt_v[:, js] = qwen_v[js, :].T
        return carry

    lax.fori_loop(0, cols // 256, turn, 0)

    def spread(lhs, dense, tiles):
        high = dense.astype(jnp.bfloat16).astype(jnp.float32)
        rest = dense - high
        for t in range(tiles):
            lhs[0:1, t * LANES:(t + 1) * LANES] = high[t:t + 1, :]
            lhs[1:2, t * LANES:(t + 1) * LANES] = rest[t:t + 1, :]

    half = col_tiles // 16 * 8

    def column_exchange(dest, recv_ref, k):
        a = row_lhs[...].astype(jnp.bfloat16)
        for b in range(cols // 256):
            c = jnp.sum(dot(a, kt_v[b * 256:(b + 1) * 256, :], NT), axis=0, keepdims=True)
            for h in range(2):
                dest[2 * b + h:2 * b + h + 1, :] = c[:, h * LANES:(h + 1) * LANES]
            if 2 * (b + 1) == half:
                part = pl.ds(0, half)
                start(dest.at[part], recv_ref.at[:, part], k, src_peers)
        part = pl.ds(half, dest.shape[0] - half)
        start(dest.at[part], recv_ref.at[:, part], k, src_peers)

    wait(r1_recv, recv_sem.at[0])
    top = jnp.maximum(r1_send[...], jnp.max(r1_recv[...], axis=0))
    mass = jnp.exp(r1_send[...] - top) + jnp.sum(jnp.exp(r1_recv[...] - top), axis=0)
    factor = jnp.exp(INV_TEMP * peak_v[...] - (top + jnp.log(mass)))
    spread(row_lhs, src_counts * factor, row_tiles)

    column_exchange(c1_send, c1_recv, 2)
    wait(t_recv, recv_sem.at[1])
    vocab_total = t_send[...] + jnp.sum(t_recv[...], axis=0)
    wait(c1_recv, recv_sem.at[2])
    sums = c1_send[...] + jnp.sum(c1_recv[...], axis=0)
    slab_total = sums[col_tiles:col_tiles + 1, :]
    spread(col_lhs, tgt_counts / (sums[:col_tiles, :] / slab_total + other_mass), col_tiles)

    r = jnp.sum(dot(col_lhs[...].astype(jnp.bfloat16), kt_v[...], NN), axis=0, keepdims=True)
    for t in range(row_tiles):
        r2_send[t:t + 1, :] = r[:, t * LANES:(t + 1) * LANES] * factor[t:t + 1, :]
    start(r2_send, r2_recv, 3, tgt_peers)
    wait(r2_recv, recv_sem.at[3])
    gain = factor / (r2_send[...] + jnp.sum(r2_recv[...], axis=0))
    gain_v[...] = gain
    spread(row_lhs, src_counts / slab_total * vocab_total * gain, row_tiles)

    column_exchange(c2_send, c2_recv, 4)
    wait(c2_recv, recv_sem.at[4])
    sums = c2_send[...] + jnp.sum(c2_recv[...], axis=0)
    spread(col_lhs, tgt_counts / (sums + other_mass), col_tiles)

    for b in range(n_blocks):
        js = slice(b * block, (b + 1) * block)
        v = col_lhs[0:1, js] + col_lhs[1:2, js]
        qt_v[:, js] = (qt_v[:, js].astype(jnp.float32) * v).astype(jnp.bfloat16)

    order = sorted(range(n_parts), key=lambda k: -hops(k, n_parts))
    pair_of = [(me_z // 2 + d) % n_parts for d in order]
    n_first = f_recv.shape[0]
    side = me_z % 2
    xs = sorted(range(NX), key=lambda d: -hops(d, NX))

    def transport(k):
        lanes = pl.ds(pl.multiple_of(pair_of[k] * WIDTH, WIDTH), WIDTH)
        part = dot(qt_v[...], kt_v[:, lanes], NN)
        for h in range(2):
            scale = gain_v[pl.ds(pair_of[k] * 2 + h, 1), :]
            turned = (part[:, h * LANES:(h + 1) * LANES] * scale).T
            f_send[k, h] = turned.reshape(f_send.shape[2:])

    def over_x(k):
        for d in xs[:-1]:
            x = (me_x + d) % NX
            send(f_send.at[k, :, x], f_recv.at[k, d - 1], 5, f_sem.at[k], (me_src, me_z * NX + x))

    def over_z(k):
        wait(f_recv.at[k], f_sem.at[k])
        g_send[k] = f_send[k, :, me_x] + jnp.sum(f_recv[k], axis=0)
        for h in range(2):
            owner = (me_src, (pair_of[k] * 2 + h) * NX + me_x)
            send(g_send.at[k, h], g_recv.at[2 * k + side], 6, recv_sem.at[5], owner)

    def straight(k):
        for d in xs:
            x = (me_x + d) % NX
            for h in range(2):
                if h == 0 and d == 0:
                    continue
                half = (side + h) % 2
                owner = (me_src, (pair_of[k] * 2 + half) * NX + x)
                send(f_send.at[k, half, x], d_recv.at[h * NX + d - 1], 7, recv_sem.at[6], owner)

    for k in range(n_parts):
        transport(k)
        if k < n_first:
            over_x(k)
    for k in range(n_first):
        if k == n_first - 1:
            straight(n_parts - 1)
        over_z(k)

    wait(g_recv, recv_sem.at[5])
    wait(d_recv, recv_sem.at[6])
    total = f_send[n_parts - 1, side, me_x] + jnp.sum(d_recv[...], axis=0)
    out_ref[...] = total + jnp.sum(g_recv[...], axis=0)

    sent = (r1_recv, t_recv, c1_recv, r2_recv, c2_recv, f_recv, g_recv, d_recv)
    for k, ref in enumerate(sent):
        wait(ref, send_sem.at[k])


def on_device(n_src, n_tgt, src_embed, tgt_embed, qwen_embed, other_log, src_counts, tgt_counts):
    rows, emb = src_embed.shape
    cols, dim = qwen_embed.shape
    row_tiles, col_tiles = rows // LANES, cols // LANES
    owned, n_z, n_parts = rows // n_tgt, n_tgt // NX, rows // WIDTH
    assert owned * NX == LANES and n_parts * 2 == n_z
    n_first = n_parts - 1
    f32, bf16 = jnp.float32, jnp.bfloat16
    vmem = pl.BlockSpec(memory_space=pltpu.VMEM)
    hbm = pl.BlockSpec(memory_space=pltpu.HBM)
    return pl.pallas_call(
        functools.partial(kernel, n_src, n_tgt),
        out_shape=jax.ShapeDtypeStruct((owned, dim), f32),
        in_specs=[hbm] * 6,
        out_specs=vmem,
        scratch_shapes=[
            pltpu.VMEM((col_tiles, LANES), f32),
            pltpu.VMEM((row_tiles, LANES), jnp.int32),
            pltpu.VMEM((col_tiles, LANES), jnp.int32),
            pltpu.VMEM((rows, emb), bf16),
            pltpu.VMEM((cols, emb), bf16),
            pltpu.VMEM((cols, dim), bf16),
            pltpu.VMEM((dim, cols), bf16),
            pltpu.VMEM((cols, min(512, rows)), f32),
            pltpu.VMEM((cols, min(512, rows)), f32),
            pltpu.VMEM((cols, rows), bf16),
            pltpu.VMEM((8, rows), f32),
            pltpu.VMEM((8, cols), f32),
            pltpu.VMEM((row_tiles, LANES), f32),
            pltpu.VMEM((row_tiles, LANES), f32),
            pltpu.VMEM((row_tiles, LANES), f32),
            pltpu.VMEM((n_tgt - 1, row_tiles, LANES), f32),
            pltpu.VMEM((1, LANES), f32),
            pltpu.VMEM((n_tgt - 1, 1, LANES), f32),
            pltpu.VMEM((col_tiles + 2, LANES), f32),
            pltpu.VMEM((n_src - 1, col_tiles + 2, LANES), f32),
            pltpu.VMEM((row_tiles, LANES), f32),
            pltpu.VMEM((n_tgt - 1, row_tiles, LANES), f32),
            pltpu.VMEM((col_tiles, LANES), f32),
            pltpu.VMEM((n_src - 1, col_tiles, LANES), f32),
            pltpu.VMEM((n_parts, 2, NX, owned, dim), f32),
            pltpu.VMEM((n_first, NX - 1, 2, owned, dim), f32),
            pltpu.VMEM((n_first, 2, owned, dim), f32),
            pltpu.VMEM((2 * n_first, owned, dim), f32),
            pltpu.VMEM((2 * NX - 1, owned, dim), f32),
            pltpu.SemaphoreType.DMA((9,)),
            pltpu.SemaphoreType.DMA((8,)),
            pltpu.SemaphoreType.DMA((7,)),
            pltpu.SemaphoreType.DMA((n_first,)),
        ],
        compiler_params=pltpu.CompilerParams(
            collective_id=0, has_side_effects=True, vmem_limit_bytes=56 * 1024 * 1024
        ),
    )(
        src_embed, tgt_embed, qwen_embed,
        other_log.reshape(col_tiles, LANES),
        src_counts.reshape(row_tiles, LANES),
        tgt_counts.reshape(col_tiles, LANES),
    )


def solution(mesh):
    return jax.shard_map(
        functools.partial(on_device, mesh.shape["src"], mesh.shape["tgt"]),
        mesh=mesh,
        in_specs=(P("src", None), P("tgt", None), P("tgt", None), P("tgt"), P("src"), P("tgt")),
        out_specs=P(("src", "tgt"), None),
        check_vma=False,
    )
```

```python
import functools
import math

import jax
import jax.numpy as jnp
from jax import lax
from jax.experimental import pallas as pl
from jax.experimental.pallas import tpu as pltpu
from jax.sharding import PartitionSpec as P

MESH = pl.DeviceIdType.MESH
LANES = 128
WIDTH = 256
NX = 4
INV_TEMP = 4.0
SCALE = INV_TEMP * math.log2(math.e)
NT = (((1,), (1,)), ((), ()))
NN = (((1,), (0,)), ((), ()))


def dot(a, b, dims):
    return lax.dot_general(a, b, dims, preferred_element_type=jnp.float32)


def hops(d, n):
    return min(d, n - d)


def kernel(
    n_src, n_tgt,
    src_hbm, tgt_hbm, qwen_hbm, other_hbm, src_counts_hbm, tgt_counts_hbm,
    out_ref,
    other_ref, src_counts_ref, tgt_counts_ref, src_v, tgt_v, qwen_v, qt_v, logit_a, logit_b, kt_v, row_lhs, col_lhs, peak_v, gain_v,
    r1_send, r1_recv, t_send, t_recv, c1_send, c1_recv, r2_send, r2_recv, c2_send, c2_recv,
    f_send, f_recv, g_send, g_recv, d_recv,
    load_sem, send_sem, recv_sem, f_sem,
):
    rows = src_v.shape[0]
    cols = tgt_v.shape[0]
    n_z = n_tgt // NX
    row_tiles, col_tiles = rows // LANES, cols // LANES
    n_parts = rows // WIDTH
    width = logit_a.shape[1]
    n_wide = rows // width
    me_src, me_tgt = lax.axis_index("src"), lax.axis_index("tgt")
    me_z, me_x = me_tgt // NX, me_tgt % NX

    n_blocks = 4
    block = cols // n_blocks
    step = block // 4
    wide = cols // 4

    def load_tgt(b):
        js = pl.ds(b * block, block)
        return pltpu.make_async_copy(tgt_hbm.at[js, :], tgt_v.at[js, :], load_sem.at[2 + b])

    load_src = pltpu.make_async_copy(src_hbm, src_v, load_sem.at[0])
    load_qwen = pltpu.make_async_copy(qwen_hbm, qwen_v, load_sem.at[1])
    load_src.start()
    for b in range(n_blocks):
        load_tgt(b).start()
    load_small = [
        pltpu.make_async_copy(src_counts_hbm, src_counts_ref, load_sem.at[6]),
        pltpu.make_async_copy(tgt_counts_hbm, tgt_counts_ref, load_sem.at[7]),
        pltpu.make_async_copy(other_hbm, other_ref, load_sem.at[8]),
    ]
    for load in load_small:
        load.start()

    far = sorted(range(1, n_tgt), key=lambda d: -hops(d // NX, n_z) - hops(d % NX, NX))
    tgt_peers = [(me_src, (me_tgt + d) % n_tgt) for d in far]
    src_peers = [
        ((me_src + d) % n_src, me_tgt)
        for d in sorted(range(1, n_src), key=lambda d: -hops(d, n_src))
    ]
    barrier = pltpu.get_barrier_semaphore()
    for peer in tgt_peers + src_peers:
        pl.semaphore_signal(barrier, inc=1, device_id=peer, device_id_type=MESH)

    def send(src, dst, k, sem, peer):
        pltpu.make_async_remote_copy(
            src_ref=src, dst_ref=dst, send_sem=send_sem.at[k], recv_sem=sem,
            device_id=peer, device_id_type=MESH,
        ).start()

    def start(send_ref, recv_ref, k, peers):
        for slot, peer in enumerate(peers):
            send(send_ref, recv_ref.at[slot], k, recv_sem.at[k], peer)

    def wait(ref, sem):
        pltpu.make_async_copy(ref, ref, sem).wait()

    load_src.wait()

    def products(logit, i, js, peak):
        d = dot(tgt_v[js, :], src_v[i * width:(i + 1) * width, :], NT)
        logit[js, :] = d
        return jnp.maximum(peak, jnp.max(d.reshape(step // 8, 8, width), axis=0))

    def exponentials(logit, i, js, peak, total):
        e = jnp.exp2((logit[js, :] - peak) * SCALE)
        kt_v[js, i * width:(i + 1) * width] = e.astype(jnp.bfloat16)
        return total + jnp.sum(e.reshape(step // 8, 8, width), axis=0)

    def steps(b, size):
        for s in range(size // step):
            yield pl.ds(pl.multiple_of(b * size + s * step, step), step)

    low = jnp.full((8, width), -3.0e38, jnp.float32)
    zero = jnp.zeros((8, width), jnp.float32)
    logits = (logit_a, logit_b)

    def first(b, peak):
        load_tgt(b).wait()
        for js in steps(b, block):
            peak = products(logits[0], 0, js, peak)
        return peak

    peak = lax.fori_loop(0, n_blocks, first, low)
    load_qwen.start()
    for i in range(n_wide):
        peak = jnp.max(peak, axis=0, keepdims=True)

        def both(b, carry, peak=peak, i=i):
            later, total = carry
            for js in steps(b, wide):
                if i + 1 < n_wide:
                    later = products(logits[(i + 1) % 2], i + 1, js, later)
                total = exponentials(logits[i % 2], i, js, peak, total)
            return later, total

        later, total = lax.fori_loop(0, 4, both, (low, zero))
        lse = INV_TEMP * peak + jnp.log(jnp.sum(total, axis=0, keepdims=True))
        for h in range(width // LANES):
            t = i * (width // LANES) + h
            peak_v[t:t + 1, :] = peak[:, h * LANES:(h + 1) * LANES]
            r1_send[t:t + 1, :] = lse[:, h * LANES:(h + 1) * LANES]
        peak = later

    pl.semaphore_wait(barrier, len(tgt_peers) + len(src_peers))
    start(r1_send, r1_recv, 0, tgt_peers)

    for load in load_small:
        load.wait()
    tgt_counts = tgt_counts_ref[...].astype(jnp.float32)
    t_send[...] = jnp.full((1, LANES), jnp.sum(tgt_counts), jnp.float32)
    other_mass = jnp.exp(other_ref[...])
    src_counts = src_counts_ref[...].astype(jnp.float32)
    row_lhs[...] = jnp.zeros_like(row_lhs)
    col_lhs[...] = jnp.zeros_like(col_lhs)
    c1_send[col_tiles:, :] = jnp.full((2, LANES), jnp.sum(src_counts), jnp.float32)
    load_qwen.wait()

    def turn(b, carry):
        js = pl.ds(pl.multiple_of(b * 256, 256), 256)
        qt_v[:, js] = qwen_v[js, :].T
        return carry

    lax.fori_loop(0, cols // 256, turn, 0)

    def spread(lhs, dense, tiles):
        high = dense.astype(jnp.bfloat16).astype(jnp.float32)
        rest = dense - high
        for t in range(tiles):
            lhs[0:1, t * LANES:(t + 1) * LANES] = high[t:t + 1, :]
            lhs[1:2, t * LANES:(t + 1) * LANES] = rest[t:t + 1, :]

    half = col_tiles // 16 * 8

    def column_exchange(dest, recv_ref, k):
        a = row_lhs[...].astype(jnp.bfloat16)
        for b in range(cols // 256):
            c = jnp.sum(dot(a, kt_v[b * 256:(b + 1) * 256, :], NT), axis=0, keepdims=True)
            for h in range(2):
                dest[2 * b + h:2 * b + h + 1, :] = c[:, h * LANES:(h + 1) * LANES]
            if 2 * (b + 1) == half:
                part = pl.ds(0, half)
                start(dest.at[part], recv_ref.at[:, part], k, src_peers)
        part = pl.ds(half, dest.shape[0] - half)
        start(dest.at[part], recv_ref.at[:, part], k, src_peers)

    wait(r1_recv, recv_sem.at[0])
    top = jnp.maximum(r1_send[...], jnp.max(r1_recv[...], axis=0))
    mass = jnp.exp(r1_send[...] - top) + jnp.sum(jnp.exp(r1_recv[...] - top), axis=0)
    factor = jnp.exp(INV_TEMP * peak_v[...] - (top + jnp.log(mass)))
    spread(row_lhs, src_counts * factor, row_tiles)

    column_exchange(c1_send, c1_recv, 2)
    start(t_send, t_recv, 1, tgt_peers)
    wait(c1_recv, recv_sem.at[2])
    sums = c1_send[...] + jnp.sum(c1_recv[...], axis=0)
    slab_total = sums[col_tiles:col_tiles + 1, :]
    spread(col_lhs, tgt_counts / (sums[:col_tiles, :] / slab_total + other_mass), col_tiles)

    r = jnp.sum(dot(col_lhs[...].astype(jnp.bfloat16), kt_v[...], NN), axis=0, keepdims=True)
    for t in range(row_tiles):
        r2_send[t:t + 1, :] = r[:, t * LANES:(t + 1) * LANES] * factor[t:t + 1, :]
    start(r2_send, r2_recv, 3, tgt_peers)
    wait(t_recv, recv_sem.at[1])
    vocab_total = t_send[...] + jnp.sum(t_recv[...], axis=0)
    wait(r2_recv, recv_sem.at[3])
    gain = factor / (r2_send[...] + jnp.sum(r2_recv[...], axis=0))
    gain_v[...] = gain
    spread(row_lhs, src_counts / slab_total * vocab_total * gain, row_tiles)

    column_exchange(c2_send, c2_recv, 4)
    wait(c2_recv, recv_sem.at[4])
    sums = c2_send[...] + jnp.sum(c2_recv[...], axis=0)
    spread(col_lhs, tgt_counts / (sums + other_mass), col_tiles)

    for b in range(n_blocks):
        js = slice(b * block, (b + 1) * block)
        v = col_lhs[0:1, js] + col_lhs[1:2, js]
        qt_v[:, js] = (qt_v[:, js].astype(jnp.float32) * v).astype(jnp.bfloat16)

    order = sorted(range(n_parts), key=lambda k: -hops(k, n_parts))
    pair_of = [(me_z // 2 + d) % n_parts for d in order]
    n_first = f_recv.shape[0]
    side = me_z % 2
    xs = sorted(range(NX), key=lambda d: -hops(d, NX))

    def transport(k):
        lanes = pl.ds(pl.multiple_of(pair_of[k] * WIDTH, WIDTH), WIDTH)
        part = dot(qt_v[...], kt_v[:, lanes], NN)
        for h in range(2):
            scale = gain_v[pl.ds(pair_of[k] * 2 + h, 1), :]
            turned = (part[:, h * LANES:(h + 1) * LANES] * scale).T
            f_send[k, h] = turned.reshape(f_send.shape[2:])

    def over_x(k):
        for d in xs[:-1]:
            x = (me_x + d) % NX
            send(f_send.at[k, :, x], f_recv.at[k, d - 1], 5, f_sem.at[k], (me_src, me_z * NX + x))

    def over_z(k):
        wait(f_recv.at[k], f_sem.at[k])
        g_send[k] = f_send[k, :, me_x] + jnp.sum(f_recv[k], axis=0)
        for h in range(2):
            owner = (me_src, (pair_of[k] * 2 + h) * NX + me_x)
            send(g_send.at[k, h], g_recv.at[2 * k + side], 6, recv_sem.at[5], owner)

    def straight(k):
        for d in xs:
            x = (me_x + d) % NX
            for h in range(2):
                if h == 0 and d == 0:
                    continue
                half = (side + h) % 2
                owner = (me_src, (pair_of[k] * 2 + half) * NX + x)
                send(f_send.at[k, half, x], d_recv.at[h * NX + d - 1], 7, recv_sem.at[6], owner)

    for k in range(n_parts):
        transport(k)
        if k < n_first:
            over_x(k)
    for k in range(n_first):
        if k == n_first - 1:
            straight(n_parts - 1)
        over_z(k)

    wait(g_recv, recv_sem.at[5])
    wait(d_recv, recv_sem.at[6])
    total = f_send[n_parts - 1, side, me_x] + jnp.sum(d_recv[...], axis=0)
    out_ref[...] = total + jnp.sum(g_recv[...], axis=0)

    sent = (r1_recv, t_recv, c1_recv, r2_recv, c2_recv, f_recv, g_recv, d_recv)
    for k, ref in enumerate(sent):
        wait(ref, send_sem.at[k])


def on_device(n_src, n_tgt, src_embed, tgt_embed, qwen_embed, other_log, src_counts, tgt_counts):
    rows, emb = src_embed.shape
    cols, dim = qwen_embed.shape
    row_tiles, col_tiles = rows // LANES, cols // LANES
    owned, n_z, n_parts = rows // n_tgt, n_tgt // NX, rows // WIDTH
    assert owned * NX == LANES and n_parts * 2 == n_z
    n_first = n_parts - 1
    f32, bf16 = jnp.float32, jnp.bfloat16
    vmem = pl.BlockSpec(memory_space=pltpu.VMEM)
    hbm = pl.BlockSpec(memory_space=pltpu.HBM)
    return pl.pallas_call(
        functools.partial(kernel, n_src, n_tgt),
        out_shape=jax.ShapeDtypeStruct((owned, dim), f32),
        in_specs=[hbm] * 6,
        out_specs=vmem,
        scratch_shapes=[
            pltpu.VMEM((col_tiles, LANES), f32),
            pltpu.VMEM((row_tiles, LANES), jnp.int32),
            pltpu.VMEM((col_tiles, LANES), jnp.int32),
            pltpu.VMEM((rows, emb), bf16),
            pltpu.VMEM((cols, emb), bf16),
            pltpu.VMEM((cols, dim), bf16),
            pltpu.VMEM((dim, cols), bf16),
            pltpu.VMEM((cols, min(512, rows)), f32),
            pltpu.VMEM((cols, min(512, rows)), f32),
            pltpu.VMEM((cols, rows), bf16),
            pltpu.VMEM((8, rows), f32),
            pltpu.VMEM((8, cols), f32),
            pltpu.VMEM((row_tiles, LANES), f32),
            pltpu.VMEM((row_tiles, LANES), f32),
            pltpu.VMEM((row_tiles, LANES), f32),
            pltpu.VMEM((n_tgt - 1, row_tiles, LANES), f32),
            pltpu.VMEM((1, LANES), f32),
            pltpu.VMEM((n_tgt - 1, 1, LANES), f32),
            pltpu.VMEM((col_tiles + 2, LANES), f32),
            pltpu.VMEM((n_src - 1, col_tiles + 2, LANES), f32),
            pltpu.VMEM((row_tiles, LANES), f32),
            pltpu.VMEM((n_tgt - 1, row_tiles, LANES), f32),
            pltpu.VMEM((col_tiles, LANES), f32),
            pltpu.VMEM((n_src - 1, col_tiles, LANES), f32),
            pltpu.VMEM((n_parts, 2, NX, owned, dim), f32),
            pltpu.VMEM((n_first, NX - 1, 2, owned, dim), f32),
            pltpu.VMEM((n_first, 2, owned, dim), f32),
            pltpu.VMEM((2 * n_first, owned, dim), f32),
            pltpu.VMEM((2 * NX - 1, owned, dim), f32),
            pltpu.SemaphoreType.DMA((9,)),
            pltpu.SemaphoreType.DMA((8,)),
            pltpu.SemaphoreType.DMA((7,)),
            pltpu.SemaphoreType.DMA((n_first,)),
        ],
        compiler_params=pltpu.CompilerParams(
            collective_id=0, has_side_effects=True, vmem_limit_bytes=56 * 1024 * 1024
        ),
    )(
        src_embed, tgt_embed, qwen_embed,
        other_log.reshape(col_tiles, LANES),
        src_counts.reshape(row_tiles, LANES),
        tgt_counts.reshape(col_tiles, LANES),
    )


def solution(mesh):
    return jax.shard_map(
        functools.partial(on_device, mesh.shape["src"], mesh.shape["tgt"]),
        mesh=mesh,
        in_specs=(P("src", None), P("tgt", None), P("tgt", None), P("tgt"), P("src"), P("tgt")),
        out_specs=P(("src", "tgt"), None),
        check_vma=False,
    )
```
